128 devices in a mesh: dp: 8 (over z, core), mp: 16 (over y, x).
Axes of the slice: x: 4, y: 4, z: 4, core: 2. Of those that a mesh axis runs over, the one named last changes fastest.
Arguments:
- stream: bfloat16 [65536, 2048], P(('dp', 'mp')), may hold values from -5.5 to 5.5
- norm_weight: float32 [2048], replicated, may hold values from 0.5 to 1.5
- query_key_weight: bfloat16 [2048, 512], P(('dp', 'mp')), may hold values from -0.25 to 0.25
- value_weight: bfloat16 [2048, 2048], P(('dp', 'mp')), may hold values from -0.125 to 0.125
- output_weight: bfloat16 [2048, 2048], P(('dp', 'mp')), may hold values from -0.5 to 0.5
- convolution_weights: float32 [3, 2048], replicated, may hold values from -2.5 to 2.5
- adapter_down_maps: bfloat16 [64, 16, 2048], P('mp'), may hold values from -0.125 to 0.125
- adapter_up_maps: bfloat16 [64, 16, 2048], P('mp'), may hold values from -1.5 to 1.5
- prompt_lengths: int32 [128, 8], P(('dp', 'mp')), may hold values from 1 to 256, 512 in all within a row
- block_adapter_index: int32 [2048], P(('dp', 'mp')), may hold values from 0 to 63, as said below
Outputs:
- hidden: bfloat16 [65536, 2048], P(('dp', 'mp'))
The draws below stay inside these ranges and needn't reach their ends.
Inputs may be any that keep to these rules, and one draw needn't show every extreme that they name: `prompt_lengths`: each row holds the lengths of one device's 8 prompts; a row sums to 512 and its largest entry is exactly 256. `block_adapter_index`: adapters k * 4 to (k + 1) * 4 - 1 sit on index k of mp. The 16 blocks of one device name adapters of any one index of mp at most 2 times; in every draw, on each index of dp, one index of mp is named exactly 2 times by every device.
All inputs are finite; a program needn't handle non-finite values.
Results may differ from the reference program's by a relative error of at most 0.0088.
Values may be sent and summed in bfloat16 or wider, within the bound.
A program may use at most 128 MiB of HBM per device.

```python
import math
import jax
import jax.numpy as jnp
import numpy as np
from jax import lax

MODEL_WIDTH = 2048
HEADS = 16
QK = 16
ADAPTER_RANK = 16
KERNEL = 3
PROMPTS = 8
BLK = 32
ADP_DEV = 4
TOK_DEV = 512
ADAPTER_COUNT = 64
TOKENS = 65536
BLK_DEV = 16
NBLK = 2048
MOST = 2
MOST_LEN = 256
N_DP = 8
N_MP = 16
DEVICES = 128


def draw_stream(key, part):
    key_base, key_rows, key_cols = jax.random.split(key, 3)
    row_scale = jnp.exp(jax.random.uniform(key_rows, (TOKENS, 1), jnp.float32, math.log(0.1), 0.0))
    base = jnp.clip(jax.random.normal(key_base, (TOKENS, MODEL_WIDTH), jnp.float32), -6.0, 6.0)
    col_scale = jnp.exp(jax.random.uniform(key_cols, (1, MODEL_WIDTH), jnp.float32, math.log(0.3), math.log(3.0)))
    return (0.3 * base * row_scale * col_scale).astype(jnp.bfloat16)


def draw_block_adapter_index(key, part):
    key_hot, key_pick, key_sub = jax.random.split(jax.random.fold_in(key, 17), 3)
    hot_group = jax.random.randint(key_hot, (N_DP,), 0, N_MP)
    hot_device = jnp.repeat(hot_group, N_MP)
    leftover = jnp.arange(MOST, N_MP * MOST, dtype=jnp.int32) // MOST

    def one_device(device_key, hot_one):
        key_choose, key_place = jax.random.split(device_key, 2)
        chosen = jax.random.permutation(key_choose, leftover)[:BLK_DEV - MOST]
        relative = jnp.concatenate([jnp.zeros((MOST,), jnp.int32), chosen])
        relative = jax.random.permutation(key_place, relative)
        return (relative + hot_one) % N_MP
    device_keys = jax.random.split(key_pick, DEVICES)
    holder = jax.vmap(one_device)(device_keys, hot_device).reshape(NBLK)
    within = jax.random.randint(key_sub, (NBLK,), 0, ADP_DEV)
    return (holder * ADP_DEV + within).astype(jnp.int32)


def levels(rng, shape, shards, smallest, high):
    loudness = 1.0
    for dim, parts in shards:
        draws = jax.random.uniform(jax.random.fold_in(jax.random.fold_in(rng, 6), dim), (parts,), jnp.float32, smallest / len(shards), high / len(shards))
        loudness = loudness * jnp.repeat(jnp.exp(draws), shape[dim] // parts).reshape((-1,) + (1,) * (len(shape) - 1 - dim))
    return loudness


def split_up(count, total, bound, lean):
    portions = [(1 << 20) // math.isqrt(grade ** lean) + 1 for grade in range(2, count + 1)]
    rest, counts = total - bound - (count - 1), [1] * (count - 1)
    while rest > 0:
        free = [i for i in range(count - 1) if counts[i] < bound]
        pool, remaining = sum([portions[i] for i in free]), rest
        for i in free:
            addition = min(bound - counts[i], max(1, remaining * portions[i] // pool), rest)
            counts[i] = counts[i] + addition
            rest = rest - addition
    return np.array([bound] + counts)


def ragged_sizes(stream_key, amount, total, limit, lean):
    if amount == 2:
        one = jax.random.randint(stream_key, (), max(1, total - limit), min(limit, total - 1) + 1)
        return jnp.stack([one, total - one])
    tallies = jnp.asarray(split_up(amount, total, limit, lean), jnp.int32)
    couples = (amount - 1) // 2
    donor, taker = tallies[1:1 + 2 * couples:2], tallies[2:2 + 2 * couples:2]
    slack = jnp.minimum(donor - 1, limit - taker)
    passed = jax.random.randint(jax.random.fold_in(stream_key, 1), (couples,), 0, 1 << 20) % (slack + 1)
    tallies = tallies.at[1:1 + 2 * couples:2].set(donor - passed).at[2:2 + 2 * couples:2].set(taker + passed)
    return tallies[jax.random.permutation(jax.random.fold_in(stream_key, 2), amount)]


def scatter_about(stream_key, extent, scale, most, shards=(), kind=jnp.bfloat16):
    array = jax.random.normal(stream_key, extent, jnp.float32) * scale
    if len(shards) > 0:
        array = levels(stream_key, extent, shards, -0.22, 0.18) * array
    return jnp.clip(array, min=-most, max=most).astype(kind)


def setup_inputs(seed: int = 0) -> dict:
    arg_keys = jax.random.split(jax.random.key(seed), 11)
    stream = draw_stream(jax.random.fold_in(arg_keys[10], 71), 0)
    norm_weight = jnp.clip(1.0 + 0.1 * jax.random.normal(arg_keys[1], (MODEL_WIDTH,), jnp.float32), 0.5, 1.5)
    query_key_weight = scatter_about(arg_keys[2], (MODEL_WIDTH, 2 * HEADS * QK), (MODEL_WIDTH // 4) ** -0.5, 0.25, ((0, 128),))
    value_weight = scatter_about(arg_keys[3], (MODEL_WIDTH, MODEL_WIDTH), MODEL_WIDTH ** -0.5, 0.125, ((0, 128),))
    output_weight = scatter_about(arg_keys[4], (MODEL_WIDTH, MODEL_WIDTH), (MODEL_WIDTH // 16) ** -0.5, 0.5, ((0, 128),))
    convolution_weights = scatter_about(arg_keys[5], (KERNEL, MODEL_WIDTH), 0.5, 2.5, (), jnp.float32)
    adapter_down_maps = scatter_about(arg_keys[6], (ADAPTER_COUNT, ADAPTER_RANK, MODEL_WIDTH), MODEL_WIDTH ** -0.5, 0.125, ((0, 16),))
    adapter_up_maps = scatter_about(arg_keys[7], (ADAPTER_COUNT, ADAPTER_RANK, MODEL_WIDTH), ADAPTER_RANK ** -0.5, 1.5, ((0, 16),))
    prompt_lengths = jax.vmap(lambda own: ragged_sizes(own, PROMPTS, TOK_DEV, MOST_LEN, 2))(jax.random.split(arg_keys[8], DEVICES)).reshape((DEVICES, PROMPTS)).astype(jnp.int32)
    block_adapter_index = draw_block_adapter_index(jax.random.fold_in(arg_keys[10], 71), 0)
    return {"stream": stream, "norm_weight": norm_weight, "query_key_weight": query_key_weight, "value_weight": value_weight, "output_weight": output_weight, "convolution_weights": convolution_weights, "adapter_down_maps": adapter_down_maps, "adapter_up_maps": adapter_up_maps, "prompt_lengths": prompt_lengths, "block_adapter_index": block_adapter_index}


adapter_scale = 2.0
norm_eps = 1e-05

def prompt_index(lengths, total_token_count):
    bounds = jnp.cumsum(lengths)
    position = jnp.arange(total_token_count, dtype=jnp.int32)
    return lax.optimization_barrier(jnp.sum((position[:, None] >= bounds[None, :]).astype(jnp.int32), axis=1))

def short_conv(value_matrix, tap_table, segment):
    result = tap_table[0][None, :] * value_matrix
    for offset in range(1, tap_table.shape[0]):
        earlier = jnp.concatenate([jnp.zeros((offset, value_matrix.shape[1]), jnp.float32), value_matrix[:-offset]], axis=0)
        same_prompt = jnp.concatenate([jnp.zeros((offset,), jnp.bool_), segment[offset:] == segment[:-offset]], axis=0)
        result = result + tap_table[offset][None, :] * jnp.where(same_prompt[:, None], earlier, 0.0)
    return result

def taylor_heads(query_key, mixed, segment, head_count, feature):
    total_token_count, hidden_width = mixed.shape
    head_width = hidden_width // head_count
    queries = query_key[:, :head_count * feature].reshape(total_token_count, head_count, feature).transpose(1, 0, 2)
    key_rows = query_key[:, head_count * feature:].reshape(total_token_count, head_count, feature).transpose(1, 0, 2)
    value_rows = mixed.reshape(total_token_count, head_count, head_width).transpose(1, 0, 2)
    position = jnp.arange(total_token_count, dtype=jnp.int32)
    allowed = (position[None, :] <= position[:, None]) & (segment[None, :] == segment[:, None])
    score_scale = 1.0 / math.sqrt(feature)

    def one_head(operands):
        query_one, key_one, value_one = operands
        scores = jnp.dot(query_one, key_one.T, preferred_element_type=jnp.float32) * score_scale
        weight = jnp.where(allowed, 1.0 + scores + 0.5 * scores * scores, 0.0)
        row_total = lax.optimization_barrier(jnp.sum(weight, axis=1, keepdims=True))
        numerator = jnp.dot(weight.astype(jnp.bfloat16), value_one, preferred_element_type=jnp.float32)
        return numerator / row_total
    outputs = lax.map(one_head, (queries, key_rows, value_rows))
    return outputs.transpose(1, 0, 2).reshape(total_token_count, hidden_width).astype(jnp.bfloat16)

def reference(stream, norm_weight, query_key_weight, value_weight, output_weight, convolution_weights, adapter_down_maps, adapter_up_maps, prompt_lengths, block_adapter_index):
    flattened_down = adapter_down_maps.reshape(ADAPTER_COUNT * ADAPTER_RANK, MODEL_WIDTH)
    flattened_up = adapter_up_maps.reshape(ADAPTER_COUNT * ADAPTER_RANK, MODEL_WIDTH)
    owner = jnp.arange(ADAPTER_COUNT * ADAPTER_RANK, dtype=jnp.int32) // ADAPTER_RANK

    def device_layer(operands):
        rows_in, lengths, adapters = operands
        stream_f = rows_in.astype(jnp.float32)
        mean_sq = lax.optimization_barrier(jnp.mean(stream_f * stream_f, axis=1, keepdims=True))
        normed = (stream_f * lax.rsqrt(mean_sq + norm_eps) * norm_weight[None, :]).astype(jnp.bfloat16)
        query_key = jnp.dot(normed, query_key_weight, preferred_element_type=jnp.float32).astype(jnp.bfloat16)
        plain_value_rows = jnp.dot(normed, value_weight, preferred_element_type=jnp.float32)
        token_adapter = jnp.repeat(adapters, BLK)
        low_all = lax.dot_general(normed, flattened_down, (((1,), (1,)), ((), ())), preferred_element_type=jnp.float32)
        reduced_rows = jnp.where(token_adapter[:, None] == owner[None, :], low_all, 0.0).astype(jnp.bfloat16)
        adapter_delta = (adapter_scale * jnp.dot(reduced_rows, flattened_up, preferred_element_type=jnp.float32)).astype(jnp.bfloat16)
        value_matrix = plain_value_rows + adapter_delta.astype(jnp.float32)
        segment = prompt_index(lengths, TOK_DEV)
        conv = short_conv(value_matrix, convolution_weights, segment)
        mixed = (conv * jax.nn.silu(value_matrix)).astype(jnp.bfloat16)
        attended = taylor_heads(query_key, mixed, segment, HEADS, QK)
        return (stream_f + jnp.dot(attended, output_weight, preferred_element_type=jnp.float32)).astype(jnp.bfloat16)
    blocks = (stream.reshape(DEVICES, TOK_DEV, MODEL_WIDTH), prompt_lengths, block_adapter_index.reshape(DEVICES, TOK_DEV // BLK))
    return lax.map(device_layer, blocks).reshape(TOKENS, MODEL_WIDTH)
```

```python
import heapq
import math

import jax
import jax.numpy as jnp
from jax import lax
from jax.experimental import pallas as pl
from jax.experimental.pallas import tpu as pltpu
from jax.sharding import PartitionSpec as P

MESH = pl.DeviceIdType.MESH

HEADS = 16
QK = 16


adapter_scale = 2.0
norm_eps = 1e-05


def prompt_index(lengths, total_token_count):
    bounds = jnp.cumsum(lengths)
    position = jnp.arange(total_token_count, dtype=jnp.int32)
    return jnp.sum((position[:, None] >= bounds[None, :]).astype(jnp.int32), axis=1)


def short_conv(value_matrix, tap_table, segment):
    result = tap_table[0][None, :] * value_matrix
    for offset in range(1, tap_table.shape[0]):
        earlier = jnp.concatenate(
            [jnp.zeros((offset, value_matrix.shape[1]), jnp.float32), value_matrix[:-offset]],
            axis=0,
        )
        same_prompt = jnp.concatenate(
            [jnp.zeros((offset,), jnp.bool_), segment[offset:] == segment[:-offset]], axis=0
        )
        result = result + tap_table[offset][None, :] * jnp.where(same_prompt[:, None], earlier, 0.0)
    return result


def taylor_heads(query_key, mixed, segment, head_count, feature):
    total_token_count, hidden_width = mixed.shape
    head_width = hidden_width // head_count
    queries = (
        query_key[:, : head_count * feature]
        .reshape(total_token_count, head_count, feature)
        .transpose(1, 0, 2)
    )
    key_rows = (
        query_key[:, head_count * feature :]
        .reshape(total_token_count, head_count, feature)
        .transpose(1, 0, 2)
    )
    value_rows = mixed.reshape(total_token_count, head_count, head_width).transpose(1, 0, 2)
    position = jnp.arange(total_token_count, dtype=jnp.int32)
    allowed = (position[None, :] <= position[:, None]) & (segment[None, :] == segment[:, None])
    score_scale = 1.0 / math.sqrt(feature)

    def one_head(operands):
        query_one, key_one, value_one = operands
        scores = jnp.dot(query_one, key_one.T, preferred_element_type=jnp.float32) * score_scale
        weight = jnp.where(allowed, 1.0 + scores + 0.5 * scores * scores, 0.0)
        row_total = jnp.sum(weight, axis=1, keepdims=True)
        numerator = jnp.dot(
            weight.astype(jnp.bfloat16), value_one, preferred_element_type=jnp.float32
        )
        return numerator / row_total

    outputs = lax.map(one_head, (queries, key_rows, value_rows))
    return outputs.transpose(1, 0, 2).reshape(total_token_count, hidden_width).astype(jnp.bfloat16)


ORDERS = ("xyz", "yzx", "zxy")
T = 128
EV = 16
SUBS = ((0, 0, (6, 5, 5)), (1, 0, (4, 4, 4)), (1, 12, (2, 3, 3)), (2, 0, (3, 3, 2)), (2, 8, (3, 2, 3)))


def size(sub_tiles, p, e):
    t = sub_tiles[p]*4096
    if e < 3: return t
    if e < 5: return 4*t
    if e < 7: return 2*t
    if e < 9: return 16*t
    if e < 11: return 8*t
    if e < 14: return 16*t
    return 8*t
def link(s, p, e):
    a1,a2,a3 = ORDERS[p]
    if e>=11: return "d"
    if e<3:
        if e==2: return a1+("+" if (s+p)%2==0 else "-")
        return a1+"+-"[e]
    if e<7: return a2+("+-+-")[e-3]
    return a3+("+-+-")[e-7]
def greedy(subs, rate=48e3, d2d=480e3, lat=1.6, depth=4.0, early=2):
    free = {}; arr = {}; heap = []; seq=0; order=[]; got=set(); pend=[]
    known=set()
    def rank(k):
        s,p,e=k
        return (s - (early if e<7 else 0), e, p)
    def want(k):
        if k not in known: known.add(k); pend.append(k)
    def flush(t):
        nonlocal seq
        pend.sort(key=rank)
        for k in list(pend):
            s,p,e=k; l=link(*k)
            if l!="d" and free.get(l,0)-t > depth: continue
            pend.remove(k)
            order.append(("send",)+k)
            r = d2d if e>=11 else rate
            st=max(t,free.get(l,0)); fin=st+size(subs[s],p,e)/r
            free[l]=fin
            heapq.heappush(heap,(fin+lat, seq, k)); seq+=1
    for s in range(len(subs)):
        for p in range(3):
            for e in (0,1): want((s,p,e))
    flush(0)
    while heap:
        t,_,k = heapq.heappop(heap); s,p,e=k
        arr[k]=t; got.add(k)
        order.append(("recv",)+k)
        g=lambda *es: all((s,p,x) in got for x in es)
        plus=(s+p)%2==0
        if e==0 and plus or e==1 and not plus: want((s,p,2))
        if g(0,1,2): want((s,p,3)); want((s,p,4))
        if e==3: want((s,p,5))
        if e==4: want((s,p,6))
        if g(0,1,2,3,4,5,6): want((s,p,7)); want((s,p,8)); want((s,p,11))
        if e==7: want((s,p,9)); want((s,p,12))
        if e==8: want((s,p,10)); want((s,p,13))
        if e==9: want((s,p,14))
        if e==10: want((s,p,15))
        flush(t)
    assert not pend
    n=len(subs)*3*16
    assert len(order)==2*n, (len(order),n)
    return order, arr, free


def cols_of(s, p):
    b, first, tiles = SUBS[s]
    start = first + sum(tiles[:p])
    return b, slice(start * T, (start + tiles[p]) * T)

def make_comm(bufs, send_sem, recv_sem):
    dp, mp = lax.axis_index("dp"), lax.axis_index("mp")
    me = {"x": mp % 4, "y": mp // 4, "z": dp // 2}
    core = dp % 2
    def device(axis, step):
        pos = dict(me)
        pos[axis] = (me[axis] + step) % 4
        return (pos["z"] * 2 + core, pos["y"] * 4 + pos["x"])
    partner = (me["z"] * 2 + 1 - core, mp)
    def region(s, p, spec, c):
        b, cols = cols_of(s, p)
        return bufs[b].at[spec["z"], c, spec["y"], spec["x"], :, cols]
    ALL, LOW, HIGH = slice(0, 4), slice(0, 2), slice(2, 4)
    def event(s, p, e):
        a1, a2, a3 = ORDERS[p]
        def reg(v1, v2, v3):
            return {a1: v1, a2: v2, a3: v3}
        def at(axis, step):
            return (me[axis] + step) % 4
        own = core
        if e < 3:
            fwd_plus = (s + p) % 2 == 0
            table = [
                (reg(me[a1], me[a2], me[a3]), reg(at(a1, -1), me[a2], me[a3]), device(a1, 1)),
                (reg(me[a1], me[a2], me[a3]), reg(at(a1, 1), me[a2], me[a3]), device(a1, -1)),
                (reg(at(a1, -1), me[a2], me[a3]), reg(at(a1, 2), me[a2], me[a3]), device(a1, 1)) if fwd_plus else
                (reg(at(a1, 1), me[a2], me[a3]), reg(at(a1, 2), me[a2], me[a3]), device(a1, -1)),
            ]
            sent, got, target = table[e]
        elif e < 7:
            table = [
                (reg(ALL, me[a2], me[a3]), reg(ALL, at(a2, -1), me[a3]), device(a2, 1)),
                (reg(ALL, me[a2], me[a3]), reg(ALL, at(a2, 1), me[a3]), device(a2, -1)),
                (reg(LOW, at(a2, -1), me[a3]), reg(LOW, at(a2, 2), me[a3]), device(a2, 1)),
                (reg(HIGH, at(a2, 1), me[a3]), reg(HIGH, at(a2, 2), me[a3]), device(a2, -1)),
            ]
            sent, got, target = table[e - 3]
        elif e < 11:
            table = [
                (reg(ALL, ALL, me[a3]), reg(ALL, ALL, at(a3, -1)), device(a3, 1)),
                (reg(ALL, ALL, me[a3]), reg(ALL, ALL, at(a3, 1)), device(a3, -1)),
                (reg(LOW, ALL, at(a3, -1)), reg(LOW, ALL, at(a3, 2)), device(a3, 1)),
                (reg(HIGH, ALL, at(a3, 1)), reg(HIGH, ALL, at(a3, 2)), device(a3, -1)),
            ]
            sent, got, target = table[e - 7]
        else:
            table = [reg(ALL, ALL, me[a3]), reg(ALL, ALL, at(a3, -1)), reg(ALL, ALL, at(a3, 1)), reg(LOW, ALL, at(a3, 2)), reg(HIGH, ALL, at(a3, 2))]
            return region(s, p, table[e - 11], core), region(s, p, table[e - 11], 1 - core), partner
        return region(s, p, sent, own), region(s, p, got, own), target
    def copy(s, p, e, received):
        sent, got, target = event(s, p, e)
        k = (s * 3 + p) * EV + e
        r = got if received else sent
        return pltpu.make_async_remote_copy(src_ref=r, dst_ref=r, send_sem=send_sem.at[k], recv_sem=recv_sem.at[k], device_id=target, device_id_type=MESH)
    def send(s, p, e):
        copy(s, p, e, False).start()
    def recv(s, p, e):
        copy(s, p, e, True).wait_recv()
    def finish():
        for s in range(len(SUBS)):
            for p in range(3):
                for e in range(EV):
                    copy(s, p, e, False).wait_send()
    def barrier():
        sem = pltpu.get_barrier_semaphore()
        for axis in "xyz":
            for d in (1, -1):
                pl.semaphore_signal(sem, inc=1, device_id=device(axis, d), device_id_type=MESH)
        pl.semaphore_signal(sem, inc=1, device_id=partner, device_id_type=MESH)
        pl.semaphore_wait(sem, 7)
    return me, core, send, recv, finish, barrier

def load_own(me, core, qk, v, o, down, up, bufs, sems):
    z, y, x = me["z"], me["y"], me["x"]
    A, V, O = bufs
    @pl.when(core == 0)
    def _(): pltpu.make_async_copy(down.at[z], A.at[z, core, y, x], sems.at[0]).start()
    @pl.when(core == 1)
    def _(): pltpu.make_async_copy(up.at[z], A.at[z, core, y, x], sems.at[0]).start()
    cs = [pltpu.make_async_copy(qk, V.at[z, core, y, x, :, 0:512], sems.at[1]),
     pltpu.make_async_copy(v, V.at[z, core, y, x, :, 512:2560], sems.at[2]),
     pltpu.make_async_copy(o, O.at[z, core, y, x], sems.at[3])]
    for c in cs: c.start()
    pltpu.make_async_copy(down.at[z], A.at[z, core, y, x], sems.at[0]).wait()
    for c in cs: c.wait()


SHAPES = ((4, 2, 4, 4, 16, 2048), (4, 2, 4, 4, 16, 2560), (4, 2, 4, 4, 16, 2048))


def gather_kernel(order, qk, v, o, down, up, out_a, out_v, out_o, buf_a, buf_v, buf_o, send_sem, recv_sem, local_sem):
    bufs = (buf_a, buf_v, buf_o)
    me, core, send, recv, finish, barrier = make_comm(bufs, send_sem, recv_sem)
    load_own(me, core, qk, v, o, down, up, bufs, local_sem)
    barrier()
    for kind, s, p, e in order:
        (send if kind == "send" else recv)(s, p, e)
    finish()
    copies = [pltpu.make_async_copy(b, t, local_sem.at[i]) for i, (b, t) in enumerate(zip(bufs, (out_a, out_v, out_o)))]
    for c in copies:
        c.start()
    for c in copies:
        c.wait()


def gather_all(qk, v, o, down, up):
    order = greedy([s[2] for s in SUBS], depth=50.0, early=0)[0]
    n = len(SUBS) * 3 * EV
    return pl.pallas_call(
        lambda *refs: gather_kernel(order, *refs),
        out_shape=[jax.ShapeDtypeStruct(s, jnp.bfloat16) for s in SHAPES],
        in_specs=[pl.BlockSpec(memory_space=pl.ANY)] * 5,
        out_specs=[pl.BlockSpec(memory_space=pl.ANY)] * 3,
        scratch_shapes=[pltpu.VMEM(s, jnp.bfloat16) for s in SHAPES]
        + [pltpu.SemaphoreType.DMA((n,)), pltpu.SemaphoreType.DMA((n,)), pltpu.SemaphoreType.DMA((4,))],
        compiler_params=pltpu.CompilerParams(collective_id=0, has_side_effects=True, vmem_limit_bytes=60 << 20),
        name="gather_all",
    )(qk, v, o, down, up)


def local(
    stream, norm_weight, query_key_weight, value_weight, output_weight, convolution_weights,
    adapter_down_maps, adapter_up_maps, prompt_lengths, block_adapter_index,
):
    adapters, qkv, out_w = gather_all(query_key_weight, value_weight, output_weight, adapter_down_maps, adapter_up_maps)
    tokens, width = stream.shape
    stream_f = stream.astype(jnp.float32)
    mean_sq = jnp.mean(stream_f * stream_f, axis=1, keepdims=True)
    normed = (stream_f * lax.rsqrt(mean_sq + norm_eps) * norm_weight[None, :]).astype(jnp.bfloat16)
    wide = jnp.dot(normed, qkv.reshape(2048, 2560), preferred_element_type=jnp.float32)
    query_key = wide[:, :512].astype(jnp.bfloat16)
    unit = (block_adapter_index % 4) * 2 * 16 + block_adapter_index // 4
    flat = adapters.reshape(128, 16, width)
    down = jnp.take(flat, unit, axis=0).reshape(256, width)
    up = jnp.take(flat, unit + 16, axis=0).reshape(256, width)
    low = lax.dot_general(normed, down, (((1,), (1,)), ((), ())), preferred_element_type=jnp.float32)
    keep = (jnp.arange(tokens) // 32)[:, None] == (jnp.arange(256) // 16)[None, :]
    low = jnp.where(keep, low, 0.0).astype(jnp.bfloat16)
    delta = adapter_scale * jnp.dot(low, up, preferred_element_type=jnp.float32)
    value_matrix = wide[:, 512:] + delta
    segment = prompt_index(prompt_lengths[0], tokens)
    conv = short_conv(value_matrix, convolution_weights, segment)
    mixed = (conv * jax.nn.silu(value_matrix)).astype(jnp.bfloat16)
    attended = taylor_heads(query_key, mixed, segment, HEADS, QK)
    projected = jnp.dot(attended, out_w.reshape(2048, 2048), preferred_element_type=jnp.float32)
    return (stream_f + projected).astype(jnp.bfloat16)


def solution(mesh):
    return jax.shard_map(
        local,
        mesh=mesh,
        in_specs=(
            P(("dp", "mp"), None),
            P(),
            P(("dp", "mp"), None),
            P(("dp", "mp"), None),
            P(("dp", "mp"), None),
            P(),
            P("mp", None, None),
            P("mp", None, None),
            P(("dp", "mp"), None),
            P(("dp", "mp")),
        ),
        out_specs=P(("dp", "mp"), None),
        check_vma=False,
    )
```

```python
import heapq

import jax
import jax.numpy as jnp
from jax import lax
from jax.experimental import pallas as pl
from jax.experimental.pallas import tpu as pltpu
from jax.sharding import PartitionSpec as P

MESH = pl.DeviceIdType.MESH
F32, BF16 = jnp.float32, jnp.bfloat16
HEADS = 16
QK = 16
BLK = 32
NORM_EPS = 1e-05
TOK, WIDTH = 512, 2048

ORDERS = ("xyz", "yzx", "zxy")
TILE = 128
EVENTS = 16
SHAPES = ((4, 2, 4, 4, 16, WIDTH), (4, 2, 4, 4, 16, 512 + WIDTH), (4, 2, 4, 4, 16, WIDTH))
SLABS = ((1, 0, (4, 4, 4)), (1, 12, (2, 3, 3)), (0, 0, (6, 5, 5)), (2, 0, (3, 3, 2)), (2, 8, (3, 2, 3)))


def event_bytes(tiles, part, event):
    unit = tiles[part] * 16 * TILE * 2
    return unit * (1 if event < 3 else 4 if event < 5 else 2 if event < 7 else 16 if event < 9 else 8 if event < 11 else 16 if event < 14 else 8)


def event_link(slab, part, event):
    a1, a2, a3 = ORDERS[part]
    if event >= 11:
        return "d"
    if event == 2:
        return a1 + ("+" if (slab + part) % 2 == 0 else "-")
    if event < 3:
        return a1 + "+-"[event]
    if event < 7:
        return a2 + "+-+-"[event - 3]
    return a3 + "+-+-"[event - 7]


def plan(pieces, rate=48e3, partner_rate=480e3, latency=1.6, depth=4.0, early=2, t_start=0.0):
    tiles = [s[2] for s in SLABS]
    free, arrived, heap, order, got, waiting, known = {}, {}, [], [], set(), [], set()
    left = {s: 3 * EVENTS for s in range(len(SLABS))}
    todo = list(pieces)
    state = {"seq": 0}

    def rank(k):
        return (k[0] - (early if k[2] < 7 else 0), k[2], k[1])

    def want(s, p, *events):
        for e in events:
            if (s, p, e) not in known:
                known.add((s, p, e))
                waiting.append((s, p, e))

    def flush(t):
        waiting.sort(key=rank)
        for k in list(waiting):
            link = event_link(*k)
            if link != "d" and free.get(link, 0) - t > depth:
                continue
            waiting.remove(k)
            order.append(("send",) + k)
            start = max(t, free.get(link, 0))
            end = start + event_bytes(tiles[k[0]], k[1], k[2]) / (partner_rate if k[2] >= 11 else rate)
            free[link] = end
            heapq.heappush(heap, (end + latency, state["seq"], k))
            state["seq"] += 1

    def arrive(k):
        s, p, e = k
        got.add(k)
        left[s] -= 1
        order.append(("recv",) + k)
        have = lambda *events: all((s, p, x) in got for x in events)
        if e == (0 if (s + p) % 2 == 0 else 1):
            want(s, p, 2)
        if have(0, 1, 2):
            want(s, p, 3, 4)
        if e == 3:
            want(s, p, 5)
        if e == 4:
            want(s, p, 6)
        if have(0, 1, 2, 3, 4, 5, 6):
            want(s, p, 7, 8, 11)
        if e == 7:
            want(s, p, 9, 12)
        if e == 8:
            want(s, p, 10, 13)
        if e == 9:
            want(s, p, 14)
        if e == 10:
            want(s, p, 15)

    for s in range(len(SLABS)):
        for p in range(3):
            want(s, p, 0, 1)
    t = t_start
    log = []
    while heap or waiting or todo:
        while heap and heap[0][0] <= t:
            arrive(heapq.heappop(heap)[2])
        flush(t)
        ready = [c for c in todo[:1] if all(left[s] == 0 for s in c[1])]
        if ready:
            todo.remove(ready[0])
            order.append(("run", ready[0][0]))
            log.append((round(t, 1), ready[0][0]))
            t += ready[0][2]
        elif heap:
            t = max(t, heap[0][0])
    return order, t, log


def columns_of(slab, part):
    buf, first, tiles = SLABS[slab]
    start = first + sum(tiles[:part])
    return buf, slice(start * TILE, (start + tiles[part]) * TILE)


def make_comm(bufs, send_sem, recv_sem):
    dp, mp = lax.axis_index("dp"), lax.axis_index("mp")
    me = {"x": mp % 4, "y": mp // 4, "z": dp // 2}
    core = dp % 2
    partner = (me["z"] * 2 + 1 - core, mp)
    every, low, high = slice(0, 4), slice(0, 2), slice(2, 4)

    def at(axis, step):
        return (me[axis] + step) % 4

    def device(axis, step):
        pos = dict(me)
        pos[axis] = at(axis, step)
        return (pos["z"] * 2 + core, pos["y"] * 4 + pos["x"])

    def region(slab, part, pos, which_core):
        buf, cols = columns_of(slab, part)
        return bufs[buf].at[pos["z"], which_core, pos["y"], pos["x"], :, cols]

    def event(slab, part, e):
        a1, a2, a3 = ORDERS[part]

        def pos(v1, v2, v3):
            return {a1: v1, a2: v2, a3: v3}

        if e < 2:
            step = 1 if e == 0 else -1
            sent, got, target = pos(me[a1], me[a2], me[a3]), pos(at(a1, -step), me[a2], me[a3]), device(a1, step)
        elif e == 2:
            step = 1 if (slab + part) % 2 == 0 else -1
            sent, got, target = pos(at(a1, -step), me[a2], me[a3]), pos(at(a1, 2), me[a2], me[a3]), device(a1, step)
        elif e < 5:
            step = 1 if e == 3 else -1
            sent, got, target = pos(every, me[a2], me[a3]), pos(every, at(a2, -step), me[a3]), device(a2, step)
        elif e < 7:
            step, half = (1, low) if e == 5 else (-1, high)
            sent, got, target = pos(half, at(a2, -step), me[a3]), pos(half, at(a2, 2), me[a3]), device(a2, step)
        elif e < 9:
            step = 1 if e == 7 else -1
            sent, got, target = pos(every, every, me[a3]), pos(every, every, at(a3, -step)), device(a3, step)
        elif e < 11:
            step, half = (1, low) if e == 9 else (-1, high)
            sent, got, target = pos(half, every, at(a3, -step)), pos(half, every, at(a3, 2)), device(a3, step)
        else:
            step, half = ((0, every), (-1, every), (1, every), (2, low), (2, high))[e - 11]
            where = pos(half, every, at(a3, step))
            return region(slab, part, where, core), region(slab, part, where, 1 - core), partner
        return region(slab, part, sent, core), region(slab, part, got, core), target

    def copy(slab, part, e, received):
        sent, got, target = event(slab, part, e)
        k = (slab * 3 + part) * EVENTS + e
        ref = got if received else sent
        return pltpu.make_async_remote_copy(
            src_ref=ref, dst_ref=ref, send_sem=send_sem.at[k], recv_sem=recv_sem.at[k],
            device_id=target, device_id_type=MESH,
        )

    def send(slab, part, e):
        copy(slab, part, e, False).start()

    def recv(slab, part, e):
        copy(slab, part, e, True).wait_recv()

    def finish():
        for slab in range(len(SLABS)):
            for part in range(3):
                for e in range(EVENTS):
                    copy(slab, part, e, False).wait_send()

    def barrier():
        sem = pltpu.get_barrier_semaphore()
        for axis in "xyz":
            for step in (1, -1):
                pl.semaphore_signal(sem, inc=1, device_id=device(axis, step), device_id_type=MESH)
        pl.semaphore_signal(sem, inc=1, device_id=partner, device_id_type=MESH)
        pl.semaphore_wait(sem, 7)

    return me, core, send, recv, finish, barrier


def own_copies(me, core, qk, v, o, down, up, bufs, sems):
    z, y, x = me["z"], me["y"], me["x"]
    a_buf, v_buf, o_buf = bufs
    adapter = a_buf.at[z, core, y, x]

    @pl.when(core == 0)
    def _():
        pltpu.make_async_copy(down.at[z], adapter, sems.at[0]).start()

    @pl.when(core == 1)
    def _():
        pltpu.make_async_copy(up.at[z], adapter, sems.at[0]).start()

    copies = [
        pltpu.make_async_copy(qk, v_buf.at[z, core, y, x, :, 0:512], sems.at[1]),
        pltpu.make_async_copy(v, v_buf.at[z, core, y, x, :, 512 : 512 + WIDTH], sems.at[2]),
        pltpu.make_async_copy(o, o_buf.at[z, core, y, x], sems.at[3]),
    ]
    for c in copies:
        c.start()

    def wait():
        pltpu.make_async_copy(down.at[z], adapter, sems.at[0]).wait()
        for c in copies:
            c.wait()

    return wait


def dot(a, b):
    return jnp.dot(a, b, preferred_element_type=F32)


def dot_t(a, b):
    return lax.dot_general(a, b, (((1,), (1,)), ((), ())), preferred_element_type=F32)


def kernel(
    order, lengths, adapters, stream, gain, qk, v, o, taps, down, up, out,
    a_buf, v_buf, o_buf, x_buf, normed, values, qk_buf, attended, sel_down, sel_up, low_buf, mix, mask, same,
    send_sem, recv_sem, local_sem,
):
    bufs = (a_buf, v_buf, o_buf)
    me, core, send, recv, finish, barrier = make_comm(bufs, send_sem, recv_sem)
    wait_own = own_copies(me, core, qk, v, o, down, up, bufs, local_sem)
    stream_in = pltpu.make_async_copy(stream, x_buf, local_sem.at[4])
    stream_in.start()
    wait_own()
    barrier()

    def tile(buf, start, width):
        cols = pl.ds(pl.multiple_of(start, 128), width)
        return buf[:, :, :, :, :, cols].reshape(2048, width)

    def norm():
        stream_in.wait()

        def rows(i, _):
            r = pl.ds(pl.multiple_of(i * 32, 32), 32)
            x = x_buf[r, :].astype(F32)
            mean_sq = jnp.mean(x * x, axis=1, keepdims=True)
            normed[r, :] = (x * lax.rsqrt(mean_sq + NORM_EPS) * gain[...]).astype(BF16)
            return 0

        lax.fori_loop(0, TOK // 32, rows, 0)

    def masks():
        bounds, total = [], 0
        for k in range(8):
            total = total + lengths[0, k]
            bounds.append(total)

        def rows(i, _):
            r = pl.ds(pl.multiple_of(i * 64, 64), 64)

            def start_of(width):
                t = lax.broadcasted_iota(jnp.int32, (64, width), 0) + i * 64
                first = jnp.zeros((64, width), jnp.int32)
                for b in bounds:
                    first = jnp.where(t >= b, b, first)
                return t, first

            t, first = start_of(512)
            s = lax.broadcasted_iota(jnp.int32, (64, 512), 1)
            mask[r, :] = jnp.where((s <= t) & (s >= first), 0.5, 0.0).astype(F32)
            t, first = start_of(128)
            same[0, r, :] = jnp.where(t - 1 >= first, 1.0, 0.0).astype(F32)
            same[1, r, :] = jnp.where(t - 2 >= first, 1.0, 0.0).astype(F32)
            return 0

        lax.fori_loop(0, TOK // 64, rows, 0)

    def project_qk():
        def one(i, _):
            c = pl.ds(pl.multiple_of(i * 256, 256), 256)
            qk_buf[:, c] = dot(normed[...], tile(v_buf, i * 256, 256)).astype(BF16)
            return 0

        lax.fori_loop(0, 2, one, 0)

    def project_v(first, count):
        def one(i, _):
            c = pl.ds(pl.multiple_of(i * 256, 256), 256)
            values[:, c] = dot(normed[...], tile(v_buf, 512 + i * 256, 256))
            return 0

        lax.fori_loop(first, first + count, one, 0)

    def low_rank():
        for b in range(TOK // BLK):
            a = adapters[b]
            z, m = lax.rem(a, 4), lax.div(a, 4)
            y, x = lax.div(m, 4), lax.rem(m, 4)
            sel_down[b * 16 : (b + 1) * 16, :] = a_buf[z, 0, y, x]
            sel_up[b * 16 : (b + 1) * 16, :] = a_buf[z, 1, y, x]
        low = dot_t(normed[...], sel_down[...])
        block = lax.broadcasted_iota(jnp.int32, (TOK, 256), 0) // BLK
        owner = lax.broadcasted_iota(jnp.int32, (TOK, 256), 1) // 16
        low_buf[...] = (2.0 * jnp.where(block == owner, low, 0.0)).astype(BF16)

    def heads(first, count):
        def one(h, _):
            c = pl.ds(pl.multiple_of(h * 128, 128), 128)
            val = values[:, c] + dot(low_buf[...], sel_up[:, c]).astype(BF16).astype(F32)
            conv = taps[0:1, c] * val
            conv = conv + taps[1:2, c] * (pltpu.roll(val, 1, axis=0) * same[0])
            conv = conv + taps[2:3, c] * (pltpu.roll(val, 2, axis=0) * same[1])
            mix[...] = (conv * (val / (1.0 + jnp.exp(-val)))).astype(BF16)
            group = pl.multiple_of(h // 8 * 128, 128)
            lane_head = lax.broadcasted_iota(jnp.int32, (TOK, 128), 1) // 16
            q = qk_buf[:, pl.ds(group, 128)].astype(F32)
            q = jnp.where(lane_head == h % 8, q * 0.25, 0.0).astype(BF16)
            k = qk_buf[:, pl.ds(256 + group, 128)]
            for r0, k0, k1 in ((0, 0, 128), (128, 0, 256), (256, 0, 384), (384, 128, 512)):
                u1 = dot_t(q[r0 : r0 + 128], k[k0:k1]) + 1.0
                weight = ((u1 * u1 + 1.0) * mask[r0 : r0 + 128, k0:k1]).astype(BF16)
                right = jnp.concatenate([mix[k0:k1, :], jnp.ones((k1 - k0, 128), BF16)], axis=1)
                both = dot(weight, right)
                attended[r0 : r0 + 128, c] = (both[:, :128] / both[:, 128:]).astype(BF16)
            return 0

        lax.fori_loop(first, first + count, one, 0)

    out_copies = []

    def project_out(first, count):
        def one(i, _):
            c = pl.ds(pl.multiple_of(i * 256, 256), 256)
            x_buf[:, c] = (x_buf[:, c].astype(F32) + dot(attended[...], tile(o_buf, i * 256, 256))).astype(BF16)
            return 0

        lax.fori_loop(first, first + count, one, 0)
        c = slice(first * 256, (first + count) * 256)
        done = pltpu.make_async_copy(x_buf.at[:, c], out.at[:, c], local_sem.at[5 + len(out_copies)])
        done.start()
        out_copies.append(done)

    run = {"norm": norm, "masks": masks, "qk": project_qk, "low": low_rank}
    for op in order:
        if op[0] == "send":
            send(*op[1:])
        elif op[0] == "recv":
            recv(*op[1:])
        elif op[1] in run:
            run[op[1]]()
        else:
            {"v": project_v, "h": heads, "o": project_out}[op[1][0]](*op[1][1:])
    finish()
    for c in out_copies:
        c.wait()


PIECES = [
    ("norm", (), 2.0),
    ("masks", (), 0.7),
    ("qk", (0,), 1.6),
    (("v", 0, 2), (0,), 1.6),
    (("v", 2, 2), (0,), 1.6),
    (("v", 4, 2), (1,), 1.6),
    (("v", 6, 2), (1,), 1.6),
    ("low", (2,), 2.0),
    (("h", 0, 4), (), 3.0),
    (("h", 4, 4), (), 3.0),
    (("h", 8, 4), (), 3.0),
    (("h", 12, 4), (), 3.0),
    (("o", 0, 4), (3,), 3.2),
    (("o", 4, 4), (4,), 3.2),
]


def local(
    stream, norm_weight, query_key_weight, value_weight, output_weight, convolution_weights,
    adapter_down_maps, adapter_up_maps, prompt_lengths, block_adapter_index,
):
    order = plan(PIECES)[0]
    n = len(SLABS) * 3 * EVENTS
    any_, smem, vmem = (pl.BlockSpec(memory_space=m) for m in (pl.ANY, pltpu.SMEM, pltpu.VMEM))
    return pl.pallas_call(
        lambda *refs: kernel(order, *refs),
        out_shape=jax.ShapeDtypeStruct((TOK, WIDTH), BF16),
        in_specs=[smem, smem, any_, vmem, any_, any_, any_, vmem, any_, any_],
        out_specs=any_,
        scratch_shapes=[pltpu.VMEM(s, BF16) for s in SHAPES]
        + [
            pltpu.VMEM((TOK, WIDTH), BF16),
            pltpu.VMEM((TOK, WIDTH), BF16),
            pltpu.VMEM((TOK, WIDTH), F32),
            pltpu.VMEM((TOK, 512), BF16),
            pltpu.VMEM((TOK, WIDTH), BF16),
            pltpu.VMEM((256, WIDTH), BF16),
            pltpu.VMEM((256, WIDTH), BF16),
            pltpu.VMEM((TOK, 256), BF16),
            pltpu.VMEM((TOK, 128), BF16),
            pltpu.VMEM((TOK, TOK), F32),
            pltpu.VMEM((2, TOK, 128), F32),
            pltpu.SemaphoreType.DMA((n,)),
            pltpu.SemaphoreType.DMA((n,)),
            pltpu.SemaphoreType.DMA((16,)),
        ],
        compiler_params=pltpu.CompilerParams(
            collective_id=0, has_side_effects=True, vmem_limit_bytes=62 << 20
        ),
        name="layer",
    )(
        prompt_lengths, block_adapter_index, stream, norm_weight.reshape(1, WIDTH), query_key_weight,
        value_weight, output_weight, convolution_weights, adapter_down_maps, adapter_up_maps,
    )


def solution(mesh):
    rows, whole = P(("dp", "mp"), None), P()
    return jax.shard_map(
        local,
        mesh=mesh,
        in_specs=(
            rows, whole, rows, rows, rows, whole, P("mp", None, None), P("mp", None, None), rows, P(("dp", "mp")),
        ),
        out_specs=rows,
        check_vma=False,
    )
```

```python
import heapq

import jax
import jax.numpy as jnp
from jax import lax
from jax.experimental import pallas as pl
from jax.experimental.pallas import tpu as pltpu
from jax.sharding import PartitionSpec as P

MESH = pl.DeviceIdType.MESH
F32, BF16 = jnp.float32, jnp.bfloat16
HEADS = 16
QK = 16
BLK = 32
NORM_EPS = 1e-05
TOK, WIDTH = 512, 2048

ORDERS = ("xyz", "yzx", "zxy")
TILE = 128


def make_events(fine):
    ev = [(1, 1, (0, 0, 0), ()), (1, -1, (0, 0, 0), ())]
    ev.append((1, 1, (-1, 0, 0), (0,)))
    if fine:
        first = {0: (), -1: (0,), 1: (1,), 2: (2,)}
        second = {0: [0, 1, 2], -1: [], 1: [], 2: []}
        for a in (0, -1, 1, 2):
            n = len(ev)
            ev.append((2, 1, (a, 0, 0), first[a]))
            ev.append((2, -1, (a, 0, 0), first[a]))
            step = 1 if a in (0, -1) else -1
            ev.append((2, step, (a, -step, 0), (n if step == 1 else n + 1,)))
            second[-1].append(n)
            second[1].append(n + 1)
            second[2].append(n + 2)
        third = {0: [0, 1, 2] + second[-1] + second[1] + second[2], -1: [], 1: [], 2: []}
        for b in (0, -1, 1, 2):
            n = len(ev)
            ev.append((3, 1, ("all", b, 0), tuple(second[b])))
            ev.append((3, -1, ("all", b, 0), tuple(second[b])))
            step = 1 if b in (0, -1) else -1
            ev.append((3, step, ("all", b, -step), (n if step == 1 else n + 1,)))
            third[-1].append(n)
            third[1].append(n + 1)
            third[2].append(n + 2)
        for c in (0, -1, 1, 2):
            ev.append((4, 0, ("all", "all", c), tuple(third[c])))
    else:
        ev.append((2, 1, ("all", 0, 0), (0, 1, 2)))
        ev.append((2, -1, ("all", 0, 0), (0, 1, 2)))
        ev.append((2, 1, ("low", -1, 0), (3,)))
        ev.append((2, -1, ("high", 1, 0), (4,)))
        stage2 = (0, 1, 2, 3, 4, 5, 6)
        ev.append((3, 1, ("low", "all", 0), stage2))
        ev.append((3, -1, ("high", "all", 0), stage2))
        ev.append((3, 1, ("high", "all", 0), stage2))
        ev.append((3, -1, ("low", "all", 0), stage2))
        ev.append((3, 1, ("low", "all", -1), (7,)))
        ev.append((3, -1, ("high", "all", 1), (8,)))
        ev.append((4, 0, ("all", "all", 0), stage2))
        ev.append((4, 0, ("all", "all", -1), (7, 9)))
        ev.append((4, 0, ("all", "all", 1), (8, 10)))
        ev.append((4, 0, ("low", "all", 2), (11,)))
        ev.append((4, 0, ("high", "all", 2), (12,)))
    return ev


EV = make_events(False)
EVENTS = len(EV)


def event_of(slab, part, e):
    stage, step, spec, needs = EV[e]
    if e == 2 and (slab + part) % 2:
        return 1, -1, (1, 0, 0), (1,)
    return stage, step, spec, needs


SHAPES = ((4, 2, 4, 4, 16, WIDTH), (4, 2, 4, 4, 16, 512 + WIDTH), (4, 2, 4, 4, 16, WIDTH))
SLABS = ((1, 0, (4, 4, 4)), (1, 12, (2, 3, 3)), (0, 0, (6, 5, 5)), (2, 0, (3, 3, 2)), (2, 8, (3, 2, 3)))


def event_bytes(slab, part, e):
    units = 1
    for s in event_of(slab, part, e)[2]:
        units *= {"all": 4, "low": 2, "high": 2}.get(s, 1)
    return units * SLABS[slab][2][part] * 16 * TILE * 2


def plan(pieces, rate=46e3, partner_rate=480e3, latency=1.8, depth=2.0, early=1):
    free, heap, order, log = {}, [], [], []
    got = [[set() for _ in range(3)] for _ in SLABS]
    waiting = [(s, p, e) for s in range(len(SLABS)) for p in range(3) for e in range(EVENTS)]
    waiting.sort(key=lambda k: (k[0] - (0, early, early, 0, 0)[EV[k[2]][0]], EV[k[2]][0], k[2], k[1]))
    todo = list(pieces)
    seq, t = 0, 0.0
    while heap or waiting or todo:
        while heap and heap[0][0] <= t:
            s, p, e = heapq.heappop(heap)[2]
            got[s][p].add(e)
            order.append(("recv", s, p, e))
        for k in list(waiting):
            s, p, e = k
            stage, step, _, needs = event_of(s, p, e)
            link = (ORDERS[p][stage - 1], step) if stage < 4 else "partner"
            if not all(n in got[s][p] for n in needs) or (stage < 4 and free.get(link, 0) - t > depth):
                continue
            waiting.remove(k)
            order.append(("send",) + k)
            end = max(t, free.get(link, 0)) + event_bytes(s, p, e) / (rate if stage < 4 else partner_rate)
            free[link] = end
            heapq.heappush(heap, (end + latency, seq, k))
            seq += 1
        if todo and all(len(got[s][p]) == EVENTS for s in todo[0][1] for p in range(3)):
            name, _, cost = todo.pop(0)
            order.append(("run", name))
            log.append((round(t, 1), name))
            t += cost
        elif heap:
            t = max(t, heap[0][0])
    return order, t, log


def columns_of(slab, part):
    buf, first, tiles = SLABS[slab]
    start = first + sum(tiles[:part])
    return buf, slice(start * TILE, (start + tiles[part]) * TILE)


def make_comm(bufs, inputs, send_sem, recv_sem):
    dp, mp = lax.axis_index("dp"), lax.axis_index("mp")
    me = {"x": mp % 4, "y": mp // 4, "z": dp // 2}
    core = dp % 2
    partner = (me["z"] * 2 + 1 - core, mp)

    def at(axis, step):
        return (me[axis] + step) % 4

    def device(axis, step):
        pos = dict(me)
        pos[axis] = at(axis, step)
        return (pos["z"] * 2 + core, pos["y"] * 4 + pos["x"])

    slices = {"all": slice(0, 4), "low": slice(0, 2), "high": slice(2, 4)}

    def region(slab, part, spec, which_core):
        buf, cols = columns_of(slab, part)
        pos = {a: slices[s] if s in slices else at(a, s) for a, s in zip(ORDERS[part], spec)}
        return bufs[buf].at[pos["z"], which_core, pos["y"], pos["x"], :, cols]

    def copy(slab, part, e, received, source=None):
        stage, step, spec, _ = event_of(slab, part, e)
        other = core
        if stage == 4:
            target, other = partner, 1 - core
        else:
            target = device(ORDERS[part][stage - 1], step)
        if received and stage < 4:
            spec = tuple(s - step if i == stage - 1 else s for i, s in enumerate(spec))
        ref = region(slab, part, spec, other if received else core)
        k = (slab * 3 + part) * EVENTS + e
        return pltpu.make_async_remote_copy(
            src_ref=ref if source is None else source, dst_ref=ref, send_sem=send_sem.at[k], recv_sem=recv_sem.at[k],
            device_id=target, device_id_type=MESH,
        )

    def send(slab, part, e):
        if event_of(slab, part, e)[2] != (0, 0, 0):
            copy(slab, part, e, False).start()
            return
        buf, cols = columns_of(slab, part)
        qk, v, o, down, up = inputs
        if buf == 0:
            for c, adapters in ((0, down), (1, up)):

                @pl.when(core == c)
                def _(adapters=adapters):
                    copy(slab, part, e, False, adapters.at[me["z"], :, cols]).start()

        elif buf == 2:
            copy(slab, part, e, False, o.at[:, cols]).start()
        elif cols.start < 512:
            copy(slab, part, e, False, qk.at[:, cols]).start()
        else:
            copy(slab, part, e, False, v.at[:, cols.start - 512 : cols.stop - 512]).start()

    def recv(slab, part, e):
        copy(slab, part, e, True).wait_recv()

    def finish():
        for slab in range(len(SLABS)):
            for part in range(3):
                for e in range(EVENTS):
                    copy(slab, part, e, False).wait_send()

    def barrier():
        sem = pltpu.get_barrier_semaphore()
        for axis in "xyz":
            for step in (1, -1):
                pl.semaphore_signal(sem, inc=1, device_id=device(axis, step), device_id_type=MESH)
        pl.semaphore_signal(sem, inc=1, device_id=partner, device_id_type=MESH)
        return lambda: pl.semaphore_wait(sem, 7)

    return me, core, send, recv, finish, barrier


def own_copies(me, core, qk, v, o, down, up, bufs, sems):
    z, y, x = me["z"], me["y"], me["x"]
    a_buf, v_buf, o_buf = bufs
    adapter = a_buf.at[z, core, y, x]

    @pl.when(core == 0)
    def _():
        pltpu.make_async_copy(down.at[z], adapter, sems.at[0]).start()

    @pl.when(core == 1)
    def _():
        pltpu.make_async_copy(up.at[z], adapter, sems.at[0]).start()

    copies = [
        pltpu.make_async_copy(qk, v_buf.at[z, core, y, x, :, 0:512], sems.at[1]),
        pltpu.make_async_copy(v, v_buf.at[z, core, y, x, :, 512 : 512 + WIDTH], sems.at[2]),
        pltpu.make_async_copy(o, o_buf.at[z, core, y, x], sems.at[3]),
    ]
    for c in copies:
        c.start()

    def wait():
        pltpu.make_async_copy(down.at[z], adapter, sems.at[0]).wait()
        for c in copies:
            c.wait()

    return wait


def dot(a, b):
    return jnp.dot(a, b, preferred_element_type=F32)


def dot_t(a, b):
    return lax.dot_general(a, b, (((1,), (1,)), ((), ())), preferred_element_type=F32)


def kernel(
    order, lengths_in, adapters_in, stream, gain_in, qk, v, o, taps_in, down, up, out,
    a_buf, v_buf, o_buf, x_buf, normed, values, qk_buf, attended, sel_down, sel_up, low_buf, mixed, mask, same,
    weights0, weights1, lengths, adapters, gain, taps, send_sem, recv_sem, local_sem,
):
    bufs = (a_buf, v_buf, o_buf)
    me, core, send, recv, finish, barrier = make_comm(bufs, (qk, v, o, down, up), send_sem, recv_sem)
    wait_neighbours = barrier()
    wait_own = own_copies(me, core, qk, v, o, down, up, bufs, local_sem)
    stream_in = pltpu.make_async_copy(stream, x_buf, local_sem.at[4])
    stream_in.start()
    small = [
        pltpu.make_async_copy(s, d, local_sem.at[5 + i])
        for i, (s, d) in enumerate(((lengths_in, lengths), (adapters_in, adapters), (gain_in, gain), (taps_in, taps)))
    ]
    for c in small:
        c.start()
    wait_neighbours()

    def tile(buf, start, width):
        cols = pl.ds(pl.multiple_of(start, 128), width)
        return buf[:, :, :, :, :, cols].reshape(2048, width)

    def norm():
        stream_in.wait()
        for c in small:
            c.wait()

        def rows(i, _):
            r = pl.ds(pl.multiple_of(i * 32, 32), 32)
            x = x_buf[r, :].astype(F32)
            mean_sq = jnp.mean(x * x, axis=1, keepdims=True)
            normed[r, :] = (x * lax.rsqrt(mean_sq + NORM_EPS) * gain[...]).astype(BF16)
            return 0

        lax.fori_loop(0, TOK // 32, rows, 0)

    def masks():
        bounds, total = [], 0
        for k in range(8):
            total = total + lengths[0, k]
            bounds.append(total)

        def rows(i, _):
            r = pl.ds(pl.multiple_of(i * 64, 64), 64)

            def start_of(width):
                t = lax.broadcasted_iota(jnp.int32, (64, width), 0) + i * 64
                first = jnp.zeros((64, width), jnp.int32)
                for b in bounds:
                    first = jnp.where(t >= b, b, first)
                return t, first

            t, first = start_of(512)
            s = lax.broadcasted_iota(jnp.int32, (64, 512), 1)
            mask[r, :] = jnp.where((s <= t) & (s >= first), 0.5, 0.0).astype(F32)
            t, first = start_of(128)
            same[0, r, :] = jnp.where(t - 1 >= first, 1.0, 0.0).astype(F32)
            same[1, r, :] = jnp.where(t - 2 >= first, 1.0, 0.0).astype(F32)
            return 0

        lax.fori_loop(0, TOK // 64, rows, 0)

    def project_qk():
        def one(i, _):
            c = pl.ds(pl.multiple_of(i * 256, 256), 256)
            qk_buf[:, c] = dot(normed[...], tile(v_buf, i * 256, 256)).astype(BF16)
            return 0

        lax.fori_loop(0, 2, one, 0)

    def project_v(first, count):
        def one(i, _):
            c = pl.ds(pl.multiple_of(i * 256, 256), 256)
            values[:, c] = dot(normed[...], tile(v_buf, 512 + i * 256, 256))
            return 0

        lax.fori_loop(first, first + count, one, 0)

    def low_rank():
        for b in range(TOK // BLK):
            a = adapters[b]
            z, m = lax.rem(a, 4), lax.div(a, 4)
            y, x = lax.div(m, 4), lax.rem(m, 4)
            sel_down[b * 16 : (b + 1) * 16, :] = a_buf[z, 0, y, x]
            sel_up[b * 16 : (b + 1) * 16, :] = a_buf[z, 1, y, x]
        low = dot_t(normed[...], sel_down[...])
        block = lax.broadcasted_iota(jnp.int32, (TOK, 256), 0) // BLK
        owner = lax.broadcasted_iota(jnp.int32, (TOK, 256), 1) // 16
        low_buf[...] = (2.0 * jnp.where(block == owner, low, 0.0)).astype(BF16)

    def gate(first, count):
        def one(i, _):
            c = pl.ds(pl.multiple_of(i * 256, 256), 256)
            fix = dot(low_buf[...], sel_up[:, c])
            for half in range(2):
                c = pl.ds(pl.multiple_of(i * 256 + half * 128, 128), 128)
                val = values[:, c] + fix[:, half * 128 : (half + 1) * 128].astype(BF16).astype(F32)
                conv = taps[0:1, c] * val
                conv = conv + taps[1:2, c] * (pltpu.roll(val, 1, axis=0) * same[0])
                conv = conv + taps[2:3, c] * (pltpu.roll(val, 2, axis=0) * same[1])
                mixed[:, c] = (conv * (val / (1.0 + jnp.exp(-val)))).astype(BF16)
            return 0

        lax.fori_loop(first, first + count, one, 0)

    blocks = ((0, 256, 256), (256, 512, 512))

    def scores(first, count):
        def one(i, _):
            group = pl.multiple_of(i // 2 * 128, 128)
            lane_head = lax.broadcasted_iota(jnp.int32, (TOK, 128), 1) // 16
            quarter = qk_buf[:, pl.ds(group, 128)] * 0.25
            k = qk_buf[:, pl.ds(256 + group, 128)]
            for n in range(4):
                h = i * 4 + n
                q = jnp.where(lane_head == h % 8, quarter, 0.0).astype(BF16)
                for (r0, r1, k1), store in zip(blocks, (weights0, weights1)):
                    u1 = dot_t(q[r0:r1], k[:k1]) + 1.0
                    store[h] = ((u1 * u1 + 1.0) * mask[r0:r1, :k1]).astype(BF16)
            return 0

        lax.fori_loop(first, first + count, one, 0)

    def attend(first, count):
        def one(i, _):
            for n in range(4):
                h = i * 4 + n
                c = pl.ds(pl.multiple_of(h * 128, 128), 128)
                right = jnp.concatenate([mixed[:, c], jnp.ones((TOK, 128), BF16)], axis=1)
                for (r0, r1, k1), store in zip(blocks, (weights0, weights1)):
                    both = dot(store[h], right[:k1])
                    attended[r0:r1, c] = (both[:, :128] / both[:, 128:]).astype(BF16)
            return 0

        lax.fori_loop(first, first + count, one, 0)

    out_copies = []

    def project_out(first, count):
        def one(i, _):
            c = pl.ds(pl.multiple_of(i * 256, 256), 256)
            x_buf[:, c] = (x_buf[:, c].astype(F32) + dot(attended[...], tile(o_buf, i * 256, 256))).astype(BF16)
            return 0

        lax.fori_loop(first, first + count, one, 0)
        c = slice(first * 256, (first + count) * 256)
        done = pltpu.make_async_copy(x_buf.at[:, c], out.at[:, c], local_sem.at[9 + len(out_copies)])
        done.start()
        out_copies.append(done)

    run = {"norm": norm, "masks": masks, "qk": project_qk, "low": low_rank}
    own_here = False
    for op in order:
        if op[0] == "send" and event_of(*op[1:])[2] != (0, 0, 0) and not own_here:
            wait_own()
            own_here = True
        if op[0] == "send":
            send(*op[1:])
        elif op[0] == "recv":
            recv(*op[1:])
        elif op[1] in run:
            run[op[1]]()
        else:
            {"v": project_v, "g": gate, "s": scores, "h": attend, "o": project_out}[op[1][0]](*op[1][1:])
    finish()
    for c in out_copies:
        c.wait()


PIECES = [
    ("norm", (), 1.5),
    ("masks", (), 0.5),
    ("qk", (0,), 1.5),
    (("v", 0, 2), (0,), 1.5),
    (("v", 2, 2), (0,), 1.5),
    (("s", 0, 2), (), 1.6),
    (("s", 2, 2), (), 1.6),
    (("v", 4, 2), (1,), 1.5),
    (("v", 6, 2), (1,), 1.5),
    ("low", (2,), 0.8),
    (("g", 0, 4), (), 1.8),
    (("h", 0, 2), (), 1.5),
    (("g", 4, 4), (), 1.8),
    (("h", 2, 2), (), 1.5),
    (("o", 0, 2), (3,), 1.7),
    (("o", 2, 2), (3,), 1.7),
    (("o", 4, 2), (4,), 1.7),
    (("o", 6, 2), (4,), 1.7),
]


def local(
    stream, norm_weight, query_key_weight, value_weight, output_weight, convolution_weights,
    adapter_down_maps, adapter_up_maps, prompt_lengths, block_adapter_index,
):
    order = plan(PIECES)[0]
    n = len(SLABS) * 3 * EVENTS
    any_, hbm = pl.BlockSpec(memory_space=pl.ANY), pl.BlockSpec(memory_space=pltpu.HBM)
    return pl.pallas_call(
        lambda *refs: kernel(order, *refs),
        out_shape=jax.ShapeDtypeStruct((TOK, WIDTH), BF16),
        in_specs=[hbm] * 10,
        out_specs=any_,
        scratch_shapes=[pltpu.VMEM(s, BF16) for s in SHAPES]
        + [
            pltpu.VMEM((TOK, WIDTH), BF16),
            pltpu.VMEM((TOK, WIDTH), BF16),
            pltpu.VMEM((TOK, WIDTH), F32),
            pltpu.VMEM((TOK, 512), BF16),
            pltpu.VMEM((TOK, WIDTH), BF16),
            pltpu.VMEM((256, WIDTH), BF16),
            pltpu.VMEM((256, WIDTH), BF16),
            pltpu.VMEM((TOK, 256), BF16),
            pltpu.VMEM((TOK, WIDTH), BF16),
            pltpu.VMEM((TOK, TOK), F32),
            pltpu.VMEM((2, TOK, 128), F32),
            pltpu.VMEM((HEADS, 256, 256), BF16),
            pltpu.VMEM((HEADS, 256, 512), BF16),
            pltpu.SMEM((1, 8), jnp.int32),
            pltpu.SMEM((TOK // BLK,), jnp.int32),
            pltpu.VMEM((1, WIDTH), F32),
            pltpu.VMEM((3, WIDTH), F32),
            pltpu.SemaphoreType.DMA((n,)),
            pltpu.SemaphoreType.DMA((n,)),
            pltpu.SemaphoreType.DMA((16,)),
        ],
        compiler_params=pltpu.CompilerParams(
            collective_id=0, has_side_effects=True, vmem_limit_bytes=51 << 20
        ),
        name="layer",
    )(*[pltpu.with_memory_space_constraint(a, pltpu.HBM) for a in (
        prompt_lengths, block_adapter_index, stream, norm_weight.reshape(1, WIDTH), query_key_weight,
        value_weight, output_weight, convolution_weights, adapter_down_maps, adapter_up_maps,
    )])


def solution(mesh):
    rows, whole = P(("dp", "mp"), None), P()
    return jax.shard_map(
        local,
        mesh=mesh,
        in_specs=(
            rows, whole, rows, rows, rows, whole, P("mp", None, None), P("mp", None, None), rows, P(("dp", "mp")),
        ),
        out_specs=rows,
        check_vma=False,
    )
```

```python
import heapq

import jax
import jax.numpy as jnp
from jax import lax
from jax.experimental import pallas as pl
from jax.experimental.pallas import tpu as pltpu
from jax.sharding import PartitionSpec as P

MESH = pl.DeviceIdType.MESH
F32, BF16 = jnp.float32, jnp.bfloat16
HEADS = 16
QK = 16
BLK = 32
NORM_EPS = 1e-05
TOK, WIDTH = 512, 2048

ORDERS = ("xyz", "yzx", "zxy")
TILE = 128


def make_events(fine):
    ev = [(1, 1, (0, 0, 0), ()), (1, -1, (0, 0, 0), ())]
    ev.append((1, 1, (-1, 0, 0), (0,)))
    if fine:
        first = {0: (), -1: (0,), 1: (1,), 2: (2,)}
        second = {0: [0, 1, 2], -1: [], 1: [], 2: []}
        for a in (0, -1, 1, 2):
            n = len(ev)
            ev.append((2, 1, (a, 0, 0), first[a]))
            ev.append((2, -1, (a, 0, 0), first[a]))
            step = 1 if a in (0, -1) else -1
            ev.append((2, step, (a, -step, 0), (n if step == 1 else n + 1,)))
            second[-1].append(n)
            second[1].append(n + 1)
            second[2].append(n + 2)
        third = {0: [0, 1, 2] + second[-1] + second[1] + second[2], -1: [], 1: [], 2: []}
        for b in (0, -1, 1, 2):
            n = len(ev)
            ev.append((3, 1, ("all", b, 0), tuple(second[b])))
            ev.append((3, -1, ("all", b, 0), tuple(second[b])))
            step = 1 if b in (0, -1) else -1
            ev.append((3, step, ("all", b, -step), (n if step == 1 else n + 1,)))
            third[-1].append(n)
            third[1].append(n + 1)
            third[2].append(n + 2)
        for c in (0, -1, 1, 2):
            ev.append((4, 0, ("all", "all", c), tuple(third[c])))
    else:
        ev.append((2, 1, ("all", 0, 0), (0, 1, 2)))
        ev.append((2, -1, ("all", 0, 0), (0, 1, 2)))
        ev.append((2, 1, ("low", -1, 0), (3,)))
        ev.append((2, -1, ("high", 1, 0), (4,)))
        stage2 = (0, 1, 2, 3, 4, 5, 6)
        if fine is None:
            ev.append((3, 1, ("all", "all", 0), stage2))
            ev.append((3, -1, ("all", "all", 0), stage2))
            near, far = ((7,), (8,)), (9, 10)
        else:
            ev.append((3, 1, ("low", "all", 0), stage2))
            ev.append((3, -1, ("high", "all", 0), stage2))
            ev.append((3, 1, ("high", "all", 0), stage2))
            ev.append((3, -1, ("low", "all", 0), stage2))
            near, far = ((7, 9), (8, 10)), (11, 12)
        ev.append((3, 1, ("low", "all", -1), (7,)))
        ev.append((3, -1, ("high", "all", 1), (8,)))
        ev.append((4, 0, ("all", "all", 0), stage2))
        ev.append((4, 0, ("all", "all", -1), near[0]))
        ev.append((4, 0, ("all", "all", 1), near[1]))
        ev.append((4, 0, ("low", "all", 2), far[:1]))
        ev.append((4, 0, ("high", "all", 2), far[1:]))
    return ev


EV = make_events(False)
EVENTS = len(EV)


def event_of(slab, part, e):
    stage, step, spec, needs = EV[e]
    if e == 2 and (slab + part) % 2:
        return 1, -1, (1, 0, 0), (1,)
    return stage, step, spec, needs


SHAPES = ((4, 2, 4, 4, 16, WIDTH), (4, 2, 4, 4, 16, 512 + WIDTH), (4, 2, 4, 4, 16, WIDTH))
SLABS = ((1, 0, (4, 4, 4)), (1, 12, (2, 3, 3)), (0, 0, (6, 5, 5)), (2, 0, (3, 3, 2)), (2, 8, (3, 2, 3)))


def event_bytes(slab, part, e):
    units = 1
    for s in event_of(slab, part, e)[2]:
        units *= {"all": 4, "low": 2, "high": 2}.get(s, 1)
    return units * SLABS[slab][2][part] * 16 * TILE * 2


def plan(pieces, rate=46e3, partner_rate=480e3, latency=1.8, depth=3.0, early=1):
    free, heap, order, log = {}, [], [], []
    got = [[set() for _ in range(3)] for _ in SLABS]
    waiting = [(s, p, e) for s in range(len(SLABS)) for p in range(3) for e in range(EVENTS)]
    waiting.sort(key=lambda k: (k[0] - (0, early, early, 0, 0)[EV[k[2]][0]], EV[k[2]][0], k[2], k[1]))
    todo = list(pieces)
    seq, t = 0, 0.0
    while heap or waiting or todo:
        while heap and heap[0][0] <= t:
            s, p, e = heapq.heappop(heap)[2]
            got[s][p].add(e)
            order.append(("recv", s, p, e))
        for k in list(waiting):
            s, p, e = k
            stage, step, _, needs = event_of(s, p, e)
            link = (ORDERS[p][stage - 1], step) if stage < 4 else "partner"
            if not all(n in got[s][p] for n in needs) or (stage < 4 and free.get(link, 0) - t > depth):
                continue
            waiting.remove(k)
            order.append(("send",) + k)
            end = max(t, free.get(link, 0)) + event_bytes(s, p, e) / (rate if stage < 4 else partner_rate)
            free[link] = end
            heapq.heappush(heap, (end + latency, seq, k))
            seq += 1
        if todo and all(len(got[s][p]) == EVENTS for s in todo[0][1] for p in range(3)):
            name, _, cost = todo.pop(0)
            order.append(("run", name))
            log.append((round(t, 1), name))
            t += cost
        elif heap:
            t = max(t, heap[0][0])
    return order, t, log


def columns_of(slab, part):
    buf, first, tiles = SLABS[slab]
    start = first + sum(tiles[:part])
    return buf, slice(start * TILE, (start + tiles[part]) * TILE)


def make_comm(bufs, inputs, send_sem, recv_sem):
    dp, mp = lax.axis_index("dp"), lax.axis_index("mp")
    me = {"x": mp % 4, "y": mp // 4, "z": dp // 2}
    core = dp % 2
    partner = (me["z"] * 2 + 1 - core, mp)

    def at(axis, step):
        return (me[axis] + step) % 4

    def device(axis, step):
        pos = dict(me)
        pos[axis] = at(axis, step)
        return (pos["z"] * 2 + core, pos["y"] * 4 + pos["x"])

    slices = {"all": slice(0, 4), "low": slice(0, 2), "high": slice(2, 4)}

    def region(slab, part, spec, which_core):
        buf, cols = columns_of(slab, part)
        pos = {a: slices[s] if s in slices else at(a, s) for a, s in zip(ORDERS[part], spec)}
        return bufs[buf].at[pos["z"], which_core, pos["y"], pos["x"], :, cols]

    def copy(slab, part, e, received, source=None):
        stage, step, spec, _ = event_of(slab, part, e)
        other = core
        if stage == 4:
            target, other = partner, 1 - core
        else:
            target = device(ORDERS[part][stage - 1], step)
        if received and stage < 4:
            spec = tuple(s - step if i == stage - 1 else s for i, s in enumerate(spec))
        ref = region(slab, part, spec, other if received else core)
        k = (slab * 3 + part) * EVENTS + e
        return pltpu.make_async_remote_copy(
            src_ref=ref if source is None else source, dst_ref=ref, send_sem=send_sem.at[k], recv_sem=recv_sem.at[k],
            device_id=target, device_id_type=MESH,
        )

    def send(slab, part, e):
        if event_of(slab, part, e)[2] != (0, 0, 0):
            copy(slab, part, e, False).start()
            return
        buf, cols = columns_of(slab, part)
        qk, v, o, down, up = inputs
        if buf == 0:
            for c, adapters in ((0, down), (1, up)):

                @pl.when(core == c)
                def _(adapters=adapters):
                    copy(slab, part, e, False, adapters.at[me["z"], :, cols]).start()

        elif buf == 2:
            copy(slab, part, e, False, o.at[:, cols]).start()
        elif cols.start < 512:
            copy(slab, part, e, False, qk.at[:, cols]).start()
        else:
            copy(slab, part, e, False, v.at[:, cols.start - 512 : cols.stop - 512]).start()

    def recv(slab, part, e):
        copy(slab, part, e, True).wait_recv()

    def finish():
        for slab in range(len(SLABS)):
            for part in range(3):
                for e in range(EVENTS):
                    copy(slab, part, e, False).wait_send()

    def barrier():
        sem = pltpu.get_barrier_semaphore()
        for axis in "xyz":
            for step in (1, -1):
                pl.semaphore_signal(sem, inc=1, device_id=device(axis, step), device_id_type=MESH)
        pl.semaphore_signal(sem, inc=1, device_id=partner, device_id_type=MESH)
        return lambda: pl.semaphore_wait(sem, 7)

    return me, core, send, recv, finish, barrier


def own_copies(me, core, qk, v, o, down, up, bufs, sems):
    z, y, x = me["z"], me["y"], me["x"]
    a_buf, v_buf, o_buf = bufs
    adapter = a_buf.at[z, core, y, x]

    @pl.when(core == 0)
    def _():
        pltpu.make_async_copy(down.at[z], adapter, sems.at[0]).start()

    @pl.when(core == 1)
    def _():
        pltpu.make_async_copy(up.at[z], adapter, sems.at[0]).start()

    copies = [
        pltpu.make_async_copy(qk, v_buf.at[z, core, y, x, :, 0:512], sems.at[1]),
        pltpu.make_async_copy(v, v_buf.at[z, core, y, x, :, 512 : 512 + WIDTH], sems.at[2]),
        pltpu.make_async_copy(o, o_buf.at[z, core, y, x], sems.at[3]),
    ]
    for c in copies:
        c.start()

    def wait():
        pltpu.make_async_copy(down.at[z], adapter, sems.at[0]).wait()
        for c in copies:
            c.wait()

    return wait


def dot(a, b):
    return jnp.dot(a, b, preferred_element_type=F32)


def dot_t(a, b):
    return lax.dot_general(a, b, (((1,), (1,)), ((), ())), preferred_element_type=F32)


def kernel(
    order, lengths_in, adapters_in, stream, gain_in, qk, v, o, taps_in, down, up, out,
    a_buf, v_buf, o_buf, x_buf, normed, values, qk_buf, attended, sel_down, sel_up, low_buf, mixed, mask, same,
    weights0, weights1, lengths, adapters, gain, taps, send_sem, recv_sem, local_sem,
):
    bufs = (a_buf, v_buf, o_buf)
    me, core, send, recv, finish, barrier = make_comm(bufs, (qk, v, o, down, up), send_sem, recv_sem)
    wait_neighbours = barrier()
    wait_own = own_copies(me, core, qk, v, o, down, up, bufs, local_sem)
    stream_in = pltpu.make_async_copy(stream, x_buf, local_sem.at[4])
    stream_in.start()
    small = [
        pltpu.make_async_copy(s, d, local_sem.at[5 + i])
        for i, (s, d) in enumerate(((lengths_in, lengths), (adapters_in, adapters), (gain_in, gain), (taps_in, taps)))
    ]
    for c in small:
        c.start()
    wait_neighbours()

    def tile(buf, start, width):
        cols = pl.ds(pl.multiple_of(start, 128), width)
        return buf[:, :, :, :, :, cols].reshape(2048, width)

    def norm():
        stream_in.wait()
        for c in small:
            c.wait()

        def rows(i, _):
            r = pl.ds(pl.multiple_of(i * 32, 32), 32)
            x = x_buf[r, :].astype(F32)
            mean_sq = jnp.mean(x * x, axis=1, keepdims=True)
            normed[r, :] = (x * lax.rsqrt(mean_sq + NORM_EPS) * gain[...]).astype(BF16)
            return 0

        lax.fori_loop(0, TOK // 32, rows, 0)

    def masks():
        bounds, total = [], 0
        for k in range(8):
            total = total + lengths[0, k]
            bounds.append(total)

        def rows(i, _):
            r = pl.ds(pl.multiple_of(i * 64, 64), 64)

            def start_of(width):
                t = lax.broadcasted_iota(jnp.int32, (64, width), 0) + i * 64
                first = jnp.zeros((64, width), jnp.int32)
                for b in bounds:
                    first = jnp.where(t >= b, b, first)
                return t, first

            t, first = start_of(512)
            s = lax.broadcasted_iota(jnp.int32, (64, 512), 1)
            mask[r, :] = jnp.where((s <= t) & (s >= first), 0.5, 0.0).astype(F32)
            t, first = start_of(128)
            same[0, r, :] = jnp.where(t - 1 >= first, 1.0, 0.0).astype(F32)
            same[1, r, :] = jnp.where(t - 2 >= first, 1.0, 0.0).astype(F32)
            return 0

        lax.fori_loop(0, TOK // 64, rows, 0)

    def project_qk():
        def one(i, _):
            c = pl.ds(pl.multiple_of(i * 256, 256), 256)
            qk_buf[:, c] = dot(normed[...], tile(v_buf, i * 256, 256)).astype(BF16)
            return 0

        lax.fori_loop(0, 2, one, 0)

    def project_v(first, count):
        def one(i, _):
            c = pl.ds(pl.multiple_of(i * 256, 256), 256)
            values[:, c] = dot(normed[...], tile(v_buf, 512 + i * 256, 256))
            return 0

        lax.fori_loop(first, first + count, one, 0)

    def low_rank():
        for b in range(TOK // BLK):
            a = adapters[b]
            z, m = lax.rem(a, 4), lax.div(a, 4)
            y, x = lax.div(m, 4), lax.rem(m, 4)
            sel_down[b * 16 : (b + 1) * 16, :] = a_buf[z, 0, y, x]
            sel_up[b * 16 : (b + 1) * 16, :] = a_buf[z, 1, y, x]
        low = dot_t(normed[...], sel_down[...])
        block = lax.broadcasted_iota(jnp.int32, (TOK, 256), 0) // BLK
        owner = lax.broadcasted_iota(jnp.int32, (TOK, 256), 1) // 16
        low_buf[...] = (2.0 * jnp.where(block == owner, low, 0.0)).astype(BF16)

    def gate(first, count):
        def one(i, _):
            c = pl.ds(pl.multiple_of(i * 256, 256), 256)
            fix = dot(low_buf[...], sel_up[:, c])
            for half in range(2):
                c = pl.ds(pl.multiple_of(i * 256 + half * 128, 128), 128)
                val = values[:, c] + fix[:, half * 128 : (half + 1) * 128].astype(BF16).astype(F32)
                conv = taps[0:1, c] * val
                conv = conv + taps[1:2, c] * (pltpu.roll(val, 1, axis=0) * same[0])
                conv = conv + taps[2:3, c] * (pltpu.roll(val, 2, axis=0) * same[1])
                mixed[:, c] = (conv * (0.5 * val * (1.0 + jnp.tanh(0.5 * val)))).astype(BF16)
            return 0

        lax.fori_loop(first, first + count, one, 0)

    blocks = ((0, 256, 256), (256, 512, 512))

    def scores(first, count):
        def one(i, _):
            group = pl.multiple_of(i // 2 * 128, 128)
            lane_head = lax.broadcasted_iota(jnp.int32, (TOK, 128), 1) // 16
            quarter = qk_buf[:, pl.ds(group, 128)] * 0.25
            k = qk_buf[:, pl.ds(256 + group, 128)]
            for n in range(4):
                h = i * 4 + n
                q = jnp.where(lane_head == h % 8, quarter, 0.0).astype(BF16)
                for (r0, r1, k1), store in zip(blocks, (weights0, weights1)):
                    u1 = dot_t(q[r0:r1], k[:k1]) + 1.0
                    store[h] = ((u1 * u1 + 1.0) * mask[r0:r1, :k1]).astype(BF16)
            return 0

        lax.fori_loop(first, first + count, one, 0)

    def attend(first, count):
        def one(i, _):
            for n in range(4):
                h = i * 4 + n
                c = pl.ds(pl.multiple_of(h * 128, 128), 128)
                right = jnp.concatenate([mixed[:, c], jnp.ones((TOK, 128), BF16)], axis=1)
                for (r0, r1, k1), store in zip(blocks, (weights0, weights1)):
                    both = dot(store[h], right[:k1])
                    attended[r0:r1, c] = (both[:, :128] / both[:, 128:]).astype(BF16)
            return 0

        lax.fori_loop(first, first + count, one, 0)

    out_copies = []

    def project_out(first, count):
        def one(i, _):
            c = pl.ds(pl.multiple_of(i * 256, 256), 256)
            x_buf[:, c] = (x_buf[:, c].astype(F32) + dot(attended[...], tile(o_buf, i * 256, 256))).astype(BF16)
            return 0

        lax.fori_loop(first, first + count, one, 0)
        c = slice(first * 256, (first + count) * 256)
        done = pltpu.make_async_copy(x_buf.at[:, c], out.at[:, c], local_sem.at[9 + len(out_copies)])
        done.start()
        out_copies.append(done)

    run = {"norm": norm, "masks": masks, "qk": project_qk, "low": low_rank}
    own_here = False
    for op in order:
        if op[0] == "send" and event_of(*op[1:])[2] != (0, 0, 0) and not own_here:
            wait_own()
            own_here = True
        if op[0] == "send":
            send(*op[1:])
        elif op[0] == "recv":
            recv(*op[1:])
        elif op[1] in run:
            run[op[1]]()
        else:
            {"v": project_v, "g": gate, "s": scores, "h": attend, "o": project_out}[op[1][0]](*op[1][1:])
    finish()
    for c in out_copies:
        c.wait()


PIECES = [
    ("norm", (), 1.5),
    ("masks", (), 0.5),
    ("qk", (0,), 1.5),
    (("v", 0, 2), (0,), 1.5),
    (("v", 2, 2), (0,), 1.5),
    (("s", 0, 2), (), 1.6),
    (("s", 2, 2), (), 1.6),
    (("v", 4, 2), (1,), 1.5),
    (("v", 6, 2), (1,), 1.5),
    ("low", (2,), 0.8),
    (("g", 0, 4), (), 1.8),
    (("h", 0, 2), (), 1.5),
    (("g", 4, 4), (), 1.8),
    (("h", 2, 2), (), 1.5),
    (("o", 0, 2), (3,), 1.7),
    (("o", 2, 2), (3,), 1.7),
    (("o", 4, 2), (4,), 1.7),
    (("o", 6, 2), (4,), 1.7),
]


def local(
    stream, norm_weight, query_key_weight, value_weight, output_weight, convolution_weights,
    adapter_down_maps, adapter_up_maps, prompt_lengths, block_adapter_index,
):
    order = plan(PIECES)[0]
    n = len(SLABS) * 3 * EVENTS
    any_, hbm = pl.BlockSpec(memory_space=pl.ANY), pl.BlockSpec(memory_space=pltpu.HBM)
    return pl.pallas_call(
        lambda *refs: kernel(order, *refs),
        out_shape=jax.ShapeDtypeStruct((TOK, WIDTH), BF16),
        in_specs=[hbm] * 10,
        out_specs=any_,
        scratch_shapes=[pltpu.VMEM(s, BF16) for s in SHAPES]
        + [
            pltpu.VMEM((TOK, WIDTH), BF16),
            pltpu.VMEM((TOK, WIDTH), BF16),
            pltpu.VMEM((TOK, WIDTH), F32),
            pltpu.VMEM((TOK, 512), BF16),
            pltpu.VMEM((TOK, WIDTH), BF16),
            pltpu.VMEM((256, WIDTH), BF16),
            pltpu.VMEM((256, WIDTH), BF16),
            pltpu.VMEM((TOK, 256), BF16),
            pltpu.VMEM((TOK, WIDTH), BF16),
            pltpu.VMEM((TOK, TOK), F32),
            pltpu.VMEM((2, TOK, 128), F32),
            pltpu.VMEM((HEADS, 256, 256), BF16),
            pltpu.VMEM((HEADS, 256, 512), BF16),
            pltpu.SMEM((1, 8), jnp.int32),
            pltpu.SMEM((TOK // BLK,), jnp.int32),
            pltpu.VMEM((1, WIDTH), F32),
            pltpu.VMEM((3, WIDTH), F32),
            pltpu.SemaphoreType.DMA((n,)),
            pltpu.SemaphoreType.DMA((n,)),
            pltpu.SemaphoreType.DMA((24,)),
        ],
        compiler_params=pltpu.CompilerParams(
            collective_id=0, has_side_effects=True, vmem_limit_bytes=51 << 20
        ),
        name="layer",
    )(*[pltpu.with_memory_space_constraint(a, pltpu.HBM) for a in (
        prompt_lengths, block_adapter_index, stream, norm_weight.reshape(1, WIDTH), query_key_weight,
        value_weight, output_weight, convolution_weights, adapter_down_maps, adapter_up_maps,
    )])


def solution(mesh):
    rows, whole = P(("dp", "mp"), None), P()
    return jax.shard_map(
        local,
        mesh=mesh,
        in_specs=(
            rows, whole, rows, rows, rows, whole, P("mp", None, None), P("mp", None, None), rows, P(("dp", "mp")),
        ),
        out_specs=rows,
        check_vma=False,
    )
```
